32 devices in a mesh: groups: 2 (over x), row: 16 (over z, y, core).
Axes of the slice: x: 2, y: 2, z: 4, core: 2. Of those that a mesh axis runs over, the one named last changes fastest.
Arguments:
- query_acts: bfloat16 [1024, 14336], P('groups', 'row'), parts along dimension 0, may hold values from -6 to 6
- query_grads: bfloat16 [1024, 8192], P('groups', 'row'), parts along dimension 0, may hold values from -6 to 6
- query_index: int32 [512], P('groups'), parts along dimension 0, may hold values from 0 to 511
- act_basis: bfloat16 [14336, 14336], P('row'), may hold values from -0.0625 to 0.0625
- grad_basis: bfloat16 [8192, 8192], P('row'), may hold values from -0.09375 to 0.09375
- eigenvalues: bfloat16 [8192, 14336], P(None, 'row'), may hold values from 0.019897461 to 4
- train_acts: bfloat16 [512, 14336], P(None, 'row'), may hold values from -1.5 to 1.5
- train_grads: bfloat16 [512, 8192], P(None, 'row'), may hold values from -0.0625 to 0.0625
- train_index: int32 [512], P('groups'), parts along dimension 0, may hold values from 0 to 511
Outputs:
- scores: float32 [512], P(('groups', 'row')), parts along dimension 0
The draws below stay inside these ranges and needn't reach their ends.
There are 2 independent parts, one for each index of `groups`. The reference program is written for one: setup_inputs(seed, part) draws one part's arguments, and reference() takes and returns one part's arrays. A program takes and returns all parts, laid end to end along the dimension named above; an argument that names none is the same for every part. Nothing has to cross between parts.
Inputs may be any that keep to these rules, and one draw needn't show every extreme that they name: `query_index`: rows of the stored query arrays. `train_index`: rows of the stored training arrays.
All inputs are finite; a program needn't handle non-finite values.
Results may differ from the reference program's by a relative error of at most 0.005.
Values may be sent and summed in bfloat16 or wider, within the bound.
No kernel may reach another device: no remote copies, remote signals or barrier semaphores. Data moves between devices by JAX's collectives and lax.ppermute only.
A program may use at most 128 MiB of HBM per device.

```python
import math
import jax
import jax.numpy as jnp

D = 8192
FFW = 14336
QTOK = 256
TTOK = 256
QPOOL = 512
TPOOL = 512


def set_ends(result, rng, low, high):
    place = [jax.random.randint(jax.random.fold_in(rng, axis), (), 0, length) for axis, length in enumerate(result.shape)]
    widest = result.shape.index(max(result.shape))
    neighbour = place[:widest] + [(place[widest] + 1) % result.shape[widest]] + place[widest + 1:]
    return result.at[tuple(place)].set(low).at[tuple(neighbour)].set(high)


def raised(result, stream_key, source, target, parts, factor):
    def block_of(dim):
        return (jnp.arange(result.shape[dim]) // (result.shape[dim] // parts)).reshape((-1,) + (1,) * (result.ndim - 1 - dim))

    near = jax.random.permutation(stream_key, parts)[block_of(target)]
    other_side = (block_of(target) + parts // 2) % parts
    return jnp.where((block_of(source) == near) | (block_of(source) == other_side), factor * result, result)


def shard_levels(own_key, dims, shards, low, high):
    gain = 1.0
    for axis_at, parts in shards:
        heights = jax.random.uniform(jax.random.fold_in(jax.random.fold_in(own_key, 6), axis_at), (parts,), jnp.float32, low / len(shards), high / len(shards))
        gain = gain * jnp.repeat(jnp.exp(heights), dims[axis_at] // parts).reshape((-1,) + (1,) * (len(dims) - 1 - axis_at))
    return gain


def bell_draw(own_key, dims, width, most, pieces=(), kind=jnp.bfloat16):
    array = jax.random.normal(own_key, dims, jnp.float32) * width
    if len(pieces) > 0:
        array = shard_levels(own_key, dims, pieces, -0.22, 0.18) * array
    return jnp.clip(array, min=-most, max=most).astype(kind)


def bell_draw_with(rng, dims, deviation, reach, pieces, heavy, held_as=jnp.bfloat16):
    values = deviation * jax.random.normal(rng, dims, jnp.float32)
    if pieces:
        values = values * shard_levels(rng, dims, pieces, -0.22, 0.18)
    return jnp.clip(raised(values, jax.random.fold_in(rng, 3), *heavy), -reach, reach).astype(held_as)


def setup_inputs(seed: int = 0, part: int = 0) -> dict:
    arg_keys = jax.random.split(jax.random.key(seed), 10)
    part_splits = jax.random.split(jax.random.fold_in(arg_keys[9], part), 10)
    query_acts = bell_draw(part_splits[0], (QPOOL, FFW), 1.0, 6.0, ((1, 16),))
    query_grads = bell_draw(part_splits[1], (QPOOL, D), 1.0, 6.0, ((1, 16),))
    query_index = set_ends(jax.random.randint(part_splits[2], (QTOK,), 0, QPOOL), jax.random.fold_in(part_splits[2], 1), 0, QPOOL - 1).astype(jnp.int32)
    act_basis = bell_draw_with(arg_keys[3], (FFW, FFW), FFW ** -0.5, 0.0625, ((0, 16),), (0, 1, 16, 2.0))
    grad_basis = bell_draw_with(arg_keys[4], (D, D), D ** -0.5, 0.09375, ((0, 16),), (0, 1, 16, 2.0))
    eigenvalues = jnp.clip(jnp.exp(math.log(4.0) - 5.3034575 * jax.random.uniform(arg_keys[5], (D, FFW), jnp.float32) ** shard_levels(arg_keys[5], (D, FFW), ((1, 16),), -0.2, 0.2)), 0.019897461, 4.0).astype(jnp.bfloat16)
    train_acts = bell_draw(arg_keys[6], (TPOOL, FFW), 0.25, 1.5, ((1, 16),))
    train_grads = bell_draw(arg_keys[7], (TPOOL, D), D ** -0.5, 0.0625, ((1, 16),))
    train_index = set_ends(jax.random.randint(part_splits[8], (TTOK,), 0, TPOOL), jax.random.fold_in(part_splits[8], 1), 0, TPOOL - 1).astype(jnp.int32)
    return {"query_acts": query_acts, "query_grads": query_grads, "query_index": query_index, "act_basis": act_basis, "grad_basis": grad_basis, "eigenvalues": eigenvalues, "train_acts": train_acts, "train_grads": train_grads, "train_index": train_index}


damping = 0.1


def reference(query_acts, query_grads, query_index, act_basis, grad_basis, eigenvalues, train_acts, train_grads, train_index):
    chosen_acts = jnp.take(query_acts, query_index, axis=0)
    chosen_grads = jnp.take(query_grads, query_index, axis=0)
    rotated_acts = jnp.dot(chosen_acts, act_basis, preferred_element_type=jnp.float32).astype(jnp.bfloat16)
    rotated_grads = jnp.dot(chosen_grads, grad_basis, preferred_element_type=jnp.float32).astype(jnp.bfloat16)
    gradient_tile = jnp.dot(rotated_grads.T, rotated_acts, preferred_element_type=jnp.float32) / QTOK
    scaled_tile = (gradient_tile / (eigenvalues.astype(jnp.float32) + damping)).astype(jnp.bfloat16)
    picked_acts = jnp.take(train_acts, train_index, axis=0)
    picked_grads = jnp.take(train_grads, train_index, axis=0)
    mixed = jnp.dot(picked_grads, scaled_tile, preferred_element_type=jnp.float32)
    return jnp.sum(mixed * picked_acts.astype(jnp.float32), axis=1)
```

```python
import functools
import math

import jax
import jax.numpy as jnp
import numpy as np
from jax import lax
from jax.experimental.layout import Layout, with_layout_constraint
from jax.experimental import pallas as pl
from jax.experimental.pallas import tpu as pltpu
from jax.sharding import PartitionSpec as P

damping = 0.1


def ring_of_chips(mesh):
    row = mesh.shape["row"]
    chips = row // 2
    natural = list(range(chips))
    try:
        line = mesh.devices.reshape(-1, row)[0]
        places = [tuple(line[2 * chip].coords) for chip in natural]
    except AttributeError:
        return natural
    varying = [axis for axis in range(3) if len({place[axis] for place in places}) > 1]
    if len(varying) != 2:
        return natural
    short, long = sorted(varying, key=lambda axis: len({place[axis] for place in places}))
    if len({place[short] for place in places}) != 2:
        return natural
    low = min(place[short] for place in places)
    up = sorted((c for c in natural if places[c][short] == low), key=lambda c: places[c][long])
    down = sorted((c for c in natural if places[c][short] != low), key=lambda c: -places[c][long])
    return up + down


class Plan:
    def __init__(self, mesh):
        self.row = mesh.shape["row"]
        self.ring = ring_of_chips(mesh)
        self.chips = len(self.ring)
        self.hops = self.chips // 2
        place = {chip: at for at, chip in enumerate(self.ring)}
        chips, hops = self.chips, self.hops

        def tile(position, core):
            return 2 * self.ring[position % chips] + core

        def reduce_order(position, core):
            sign = 1 - 2 * core
            order = []
            for step in range(hops):
                order.append(tile(position + sign * (hops - step), core))
                if step < hops - 1:
                    order.append(tile(position - sign * (hops - 1 - step), core))
            return order + [tile(position, core)]

        def gather_order(position, core):
            sign = 1 - 2 * core
            order = [tile(position, core)]
            for step in range(1, hops + 1):
                order.append(tile(position - sign * step, core))
                if step < hops:
                    order.append(tile(position + sign * step, core))
            return order

        rows = []
        for device in range(self.row):
            position, core = place[device // 2], device % 2
            rows.append(
                reduce_order(position, core) + gather_order(position, core)
            )
        self.table = np.asarray(rows, np.int32)
        self.swap = [(device, device ^ 1) for device in range(self.row)]
        self.ahead = []
        self.back = []
        for device in range(self.row):
            position, core = place[device // 2], device % 2
            sign = 1 - 2 * core
            self.ahead.append((device, tile(position + sign, core)))
            self.back.append((device, tile(position - sign, core)))


def send(value, pairs):
    return lax.ppermute(value, "row", pairs)


def scaled_for_half(contracted, reach):
    return 2.0 ** math.floor(math.log2(65504.0 / (contracted * reach)))


def rows_first(value):
    return with_layout_constraint(value, Layout(tuple(range(value.ndim))))


def score_tiles(table, start, grads, picked, eigen_mine, eigen_swapped, acts_mine, acts_swapped, carried):
    count = len(grads)
    height, tokens = grads[0].shape
    trained = picked[0].shape[0]
    width = acts_mine.shape[1]

    def body(table_ref, *refs):
        refs = list(refs)
        grads_refs, refs = refs[:count], refs[count:]
        picked_refs, refs = refs[:count], refs[count:]
        eigen_refs, acts_refs, refs = refs[:2], refs[2:4], refs[4:]
        carried_refs = refs[:2] if carried is not None else (None, None)
        out_refs, (grads_now, picked_now) = refs[-4:-2], refs[-2:]
        for at in range(count):

            @pl.when(pl.program_id(0) == at)
            def _(at=at):
                grads_now[...] = grads_refs[at][...]
                picked_now[...] = picked_refs[at][...]

        for eigen_ref, acts_ref, carried_ref, out_ref in zip(eigen_refs, acts_refs, carried_refs, out_refs):
            gradient = jnp.dot(grads_now[...], acts_ref[...], preferred_element_type=jnp.float32)
            eigen = eigen_ref[...].reshape(height, width).astype(jnp.float32)
            scaled = (gradient / tokens) / (eigen + damping)
            part = jnp.dot(picked_now[...], scaled.astype(jnp.bfloat16), preferred_element_type=jnp.float32)

            @pl.when(pl.program_id(0) == 0)
            def _(part=part, carried_ref=carried_ref, out_ref=out_ref):
                out_ref[...] = part if carried_ref is None else carried_ref[...] + part

            @pl.when(pl.program_id(0) > 0)
            def _(part=part, out_ref=out_ref):
                out_ref[...] = out_ref[...] + part

    def fixed(shape):
        return pl.BlockSpec(shape, lambda g, t: (0,) * len(shape))

    in_specs = [fixed((height, tokens))] * count + [fixed((trained, height))] * count
    in_specs += [
        pl.BlockSpec((height, width), lambda g, t: (t[start + g], 0)),
        pl.BlockSpec((1, height, width), lambda g, t: (t[start + g] // 2, 0, 0)),
    ]
    in_specs += [fixed((tokens, width))] * 2
    operands = [*grads, *picked, eigen_mine, eigen_swapped, acts_mine, acts_swapped]
    if carried is not None:
        in_specs += [fixed((trained, width))] * 2
        operands += carried
    return pl.pallas_call(
        body,
        grid_spec=pltpu.PrefetchScalarGridSpec(
            num_scalar_prefetch=1,
            grid=(count,),
            in_specs=in_specs,
            out_specs=[fixed((trained, width))] * 2,
            scratch_shapes=[pltpu.VMEM((height, tokens), jnp.bfloat16), pltpu.VMEM((trained, height), jnp.bfloat16)],
        ),
        out_shape=[jax.ShapeDtypeStruct((trained, width), jnp.float32)] * 2,
        cost_estimate=pl.CostEstimate(
            flops=4 * count * width * height * (tokens + trained),
            transcendentals=0,
            bytes_accessed=2 * count * height * (2 * width + tokens + trained),
        ),
    )(table, *operands)


def on_device(
    plan,
    query_acts,
    query_grads,
    query_index,
    act_basis,
    grad_basis,
    eigenvalues,
    train_acts,
    train_grads,
    train_index,
):
    chips, hops = plan.chips, plan.hops
    me = lax.axis_index("row")
    core = me % 2
    table = lax.dynamic_index_in_dim(jnp.asarray(plan.table), me, 0, keepdims=False)

    def rows(values, index):
        return values.at[index].get(mode="promise_in_bounds")

    def gather_ring(mine):
        arrived = [mine]
        ahead, back = mine, mine
        for step in range(1, hops + 1):
            ahead = send(ahead, plan.ahead)
            arrived.append(ahead)
            if step < hops:
                back = send(back, plan.back)
                arrived.append(back)
        return arrived

    class Reduction:
        def __init__(self, chosen, basis, reach):
            width = basis.shape[1] // plan.row
            self.scale = scaled_for_half(plan.row * basis.shape[0], reach)
            product = lax.dot_general(basis, chosen, (((0,), (1,)), ((), ())), preferred_element_type=jnp.float32)
            self.product = rows_first((product * self.scale).astype(jnp.float16)).reshape(chips, 2, width, -1)
            theirs = lax.dynamic_index_in_dim(self.product, 1 - core, 1, keepdims=False)
            self.swapped = send(theirs, plan.swap)
            self.ahead = self.back = None

        def tile(self, order, extras):
            chip = table[order] // 2
            width, tokens = self.product.shape[2:]
            mine = lax.dynamic_slice(self.product, (chip, core, 0, 0), (1, 1, width, tokens)).reshape(width, tokens)
            total = mine.astype(jnp.float32)
            total = total + lax.dynamic_index_in_dim(self.swapped, chip, 0, keepdims=False).astype(jnp.float32)
            for extra in extras:
                if extra is not None:
                    total = total + extra.astype(jnp.float32)
            return total

        def step(self, at):
            ahead = self.tile(2 * at, [self.ahead]).astype(jnp.float16)
            if at < hops - 1:
                back = self.tile(2 * at + 1, [self.back]).astype(jnp.float16)
                self.back = send(back, plan.back)
            self.ahead = send(ahead, plan.ahead)

        def last(self):
            return rows_first((self.tile(chips - 1, [self.ahead, self.back]) / self.scale).astype(jnp.bfloat16))

    picked_grads = gather_ring(rows(train_grads, train_index))
    tall = eigenvalues.reshape(chips, 2, -1, eigenvalues.shape[1])
    eigen_swapped = send(lax.dynamic_index_in_dim(tall, 1 - core, 1, keepdims=False), plan.swap)
    acts = Reduction(rows(query_acts, query_index), act_basis, 6 * 0.125)
    grads = Reduction(rows(query_grads, query_index), grad_basis, 6 * 0.125)
    for step in range(hops):
        acts.step(step)
        grads.step(step)
    acts_mine = acts.last().T
    acts_swapped = send(acts_mine, plan.swap)
    rotated_grads = gather_ring(grads.last())

    carried = None
    cuts = [0] + list(range(3, chips, 2)) + [chips]
    for first, end in zip(cuts[:-1], cuts[1:]):
        carried = score_tiles(
            table,
            chips + first,
            rotated_grads[first:end],
            picked_grads[first:end],
            eigenvalues,
            eigen_swapped,
            acts_mine,
            acts_swapped,
            carried,
        )
    picked_acts = rows(train_acts, train_index)
    picked_swapped = send(picked_acts, plan.swap)
    partial_scores = jnp.sum(carried[0] * picked_acts.astype(jnp.float32), axis=1) + jnp.sum(
        carried[1] * picked_swapped.astype(jnp.float32), axis=1
    )
    spread = lax.all_to_all(partial_scores.reshape(plan.row, 1, -1), "row", 0, 0)
    return jnp.sum(spread, axis=(0, 1))


def solution(mesh):
    placed = (
        P("groups", "row"),
        P("groups", "row"),
        P("groups"),
        P("row", None),
        P("row", None),
        P(None, "row"),
        P(None, "row"),
        P(None, "row"),
        P("groups"),
    )
    return jax.shard_map(
        functools.partial(on_device, Plan(mesh)),
        mesh=mesh,
        in_specs=placed,
        out_specs=P(("groups", "row")),
        check_vma=False,
    )
```
